32 devices in a mesh: groups: 2 (over y), dp: 4 (over z), layer: 2 (over x), tensor: 2 (over core).
Axes of the slice: x: 2, y: 2, z: 4, core: 2. Of those that a mesh axis runs over, the one named last changes fastest.
Arguments:
- activations: bfloat16 [2, 1536, 14336], P('layer', ('groups', 'dp'), 'tensor'), parts along dimension 1, may hold values from -6 to 6
- out_grads: bfloat16 [2, 1536, 4096], P('layer', ('groups', 'dp'), 'tensor'), parts along dimension 1, may hold values from -6 to 6
- proj_in: bfloat16 [2, 64, 14336], P('layer', None, 'tensor'), may hold values from -0.046875 to 0.046875
- proj_out: bfloat16 [2, 64, 4096], P('layer', None, 'tensor'), may hold values from -0.09375 to 0.09375
- queries: bfloat16 [2, 256, 4096], P('layer', 'dp'), may hold values from -0.0068359375 to 0.0068359375
- lengths: int32 [16], P('groups'), parts along dimension 0, may hold values from 1 to 192, 768 in all
- owner_slot: int32 [16], P('groups'), parts along dimension 0, may hold values from 0 to 7, each once
- pad_mask: int32 [1536], P(('groups', 'dp')), parts along dimension 0, may hold values 0 or 1
Outputs:
- scores: float32 [16, 256], P(('groups', 'dp'), 'layer'), parts along dimension 0
The draws below stay inside these ranges and needn't reach their ends.
There are 2 independent parts, one for each index of `groups`. The reference program is written for one: setup_inputs(seed, part) draws one part's arguments, and reference() takes and returns one part's arrays. A program takes and returns all parts, laid end to end along the dimension named above; an argument that names none is the same for every part. Nothing has to cross between parts.
Inputs may be any that keep to these rules, and one draw needn't show every extreme that they name: `owner_slot`: every output row is the row of exactly one example. The lengths sum to 768; the longest example has exactly 192 tokens.
All inputs are finite; a program needn't handle non-finite values. No bound on the sum of `pad_mask` on one device may be relied on, other than what follows from the above.
Results may differ from the reference program's by a relative error of at most 0.0051.
Values may be sent and summed in bfloat16 or wider, within the bound.
No kernel may reach another device: no remote copies, remote signals or barrier semaphores. Data moves between devices by JAX's collectives and lax.ppermute only.
A program may use at most 64 MiB of HBM per device.

```python
import math
import jax
import jax.numpy as jnp
import numpy as np
from jax import lax

D = 4096
FF = 14336
R_IN = 64
R_OUT = 64
SKETCH = 4096
QUERIES = 256
TOK_DEV = 192
LAYERS = 2
TOKENS = 768
EXAMPLES = 8
MAXLEN = 192


def plant(result, rng, smallest, top_value):
    spot = [jax.random.randint(jax.random.fold_in(rng, axis), (), 0, length) for axis, length in enumerate(result.shape)]
    longest = result.shape.index(max(result.shape))
    next_to = spot[:longest] + [(spot[longest] + 1) % result.shape[longest]] + spot[longest + 1:]
    return result.at[tuple(spot)].set(smallest).at[tuple(next_to)].set(top_value)


def block_levels(own_key, extent, cuts, low, top_value):
    level = 1.0
    for dim, parts in cuts:
        draws = jax.random.uniform(jax.random.fold_in(jax.random.fold_in(own_key, 6), dim), (parts,), jnp.float32, low / len(cuts), top_value / len(cuts))
        level = level * jnp.repeat(jnp.exp(draws), extent[dim] // parts).reshape((-1,) + (1,) * (len(extent) - 1 - dim))
    return level


def split_up(number_of, total, reach, skew):
    portions = [(1 << 20) // math.isqrt(rank ** skew) + 1 for rank in range(2, number_of + 1)]
    surplus, counts = total - reach - (number_of - 1), [1] * (number_of - 1)
    while surplus > 0:
        free = [i for i in range(number_of - 1) if counts[i] < reach]
        pool, budget = sum([portions[i] for i in free]), surplus
        for i in free:
            extra = min(reach - counts[i], max(1, budget * portions[i] // pool), surplus)
            counts[i] = counts[i] + extra
            surplus = surplus - extra
    return np.array([reach] + counts)


def ragged(rng, count, total, limit, skew):
    if count == 2:
        one = jax.random.randint(rng, (), max(1, total - limit), min(limit, total - 1) + 1)
        return jnp.stack([one, total - one])
    tallies = jnp.asarray(split_up(count, total, limit, skew), jnp.int32)
    pairs = (count - 1) // 2
    source_of, receiver = tallies[1:1 + 2 * pairs:2], tallies[2:2 + 2 * pairs:2]
    margin = jnp.minimum(source_of - 1, limit - receiver)
    shifted = jax.random.randint(jax.random.fold_in(rng, 1), (pairs,), 0, 1 << 20) % (margin + 1)
    tallies = tallies.at[1:1 + 2 * pairs:2].set(source_of - shifted).at[2:2 + 2 * pairs:2].set(receiver + shifted)
    return tallies[jax.random.permutation(jax.random.fold_in(rng, 2), count)]


def bell_draw(stream_key, dims, scale, limit, split=(), held_as=jnp.bfloat16):
    level = block_levels(stream_key, dims, split, -0.22, 0.18) if split else 1.0
    array = jax.random.normal(stream_key, dims, jnp.float32) * scale * level
    return jnp.minimum(jnp.maximum(array, -limit), limit).astype(held_as)


def setup_inputs(seed: int = 0, part: int = 0) -> dict:
    key_list = jax.random.split(jax.random.key(seed), 9)
    part_keys = jax.random.split(jax.random.fold_in(key_list[8], part), 9)
    return {
        "activations": bell_draw(part_keys[0], (LAYERS, TOKENS, FF), 1.0, 6.0, ((0, 2), (1, 4), (2, 2))),
        "out_grads": bell_draw(part_keys[1], (LAYERS, TOKENS, D), 1.0, 6.0, ((0, 2), (1, 4), (2, 2))),
        "proj_in": bell_draw(key_list[2], (LAYERS, R_IN, FF), FF ** -0.5, 0.046875, ((0, 2), (2, 2))),
        "proj_out": bell_draw(key_list[3], (LAYERS, R_OUT, D), D ** -0.5, 0.09375, ((0, 2), (2, 2))),
        "queries": bell_draw(key_list[4], (LAYERS, QUERIES, SKETCH), (LAYERS * SKETCH * TOK_DEV // 2) ** -0.5, 0.0068359375, ((0, 2), (1, 4))),
        "lengths": ragged(part_keys[5], EXAMPLES, TOKENS, MAXLEN, 2).astype(jnp.int32),
        "owner_slot": jax.random.permutation(part_keys[6], EXAMPLES).astype(jnp.int32),
        "pad_mask": plant((jax.random.randint(part_keys[7], (TOKENS,), 0, 4) < 3).astype(jnp.int32), jax.random.fold_in(part_keys[7], 1), 0, 1),
    }


def contract_last(left, right):
    return lax.dot_general(left, right, (((1,), (1,)), ((), ())), preferred_element_type=jnp.float32)


def reference(activations, out_grads, proj_in, proj_out, queries, lengths, owner_slot, pad_mask):
    example_ends = jnp.cumsum(lengths).astype(jnp.int32)
    positions = jnp.arange(TOKENS, dtype=jnp.int32)
    example_of = jnp.sum((positions[:, None] >= example_ends[None, :]).astype(jnp.int32), axis=1).astype(jnp.int32)
    slot_of = owner_slot[example_of]
    labels = jnp.arange(EXAMPLES, dtype=jnp.int32)
    member = jnp.where(slot_of[:, None] == labels[None, :], pad_mask[:, None], 0).astype(jnp.bfloat16)

    def layer_scores(operands):
        acts, grads, p_input, p_output, query_rows = operands
        act_side = contract_last(acts, p_input).astype(jnp.bfloat16)
        grad_side = contract_last(grads, p_output).astype(jnp.bfloat16)
        weighted = (member[:, :, None] * grad_side[:, None, :]).reshape(TOKENS, EXAMPLES * R_OUT)
        sketch = lax.dot_general(weighted, act_side, (((0,), (0,)), ((), ())), preferred_element_type=jnp.float32)
        sketch = sketch.reshape(EXAMPLES, SKETCH).astype(jnp.bfloat16)
        return contract_last(sketch, query_rows)

    per_layer = lax.map(layer_scores, (activations, out_grads, proj_in, proj_out, queries))
    return jnp.sum(per_layer, axis=0)
```

```python
import functools

import jax
import jax.numpy as jnp
from jax import lax
from jax.experimental import pallas as pl
from jax.experimental.pallas import tpu as pltpu
from jax.sharding import PartitionSpec as P


VMEM = pl.BlockSpec(memory_space=pltpu.VMEM)
LANES = 128


def dot_last(left, right):
    return lax.dot_general(
        left, right, (((1,), (1,)), ((), ())), preferred_element_type=jnp.float32
    )


def project_kernel(acts, grads, p_in, p_out, mask, out):
    rank = p_out.shape[1]
    keep = mask[...].astype(jnp.float32)
    out[:rank] = dot_last(p_out[0], grads[0]) * keep
    out[rank:] = dot_last(p_in[0], acts[0])


def project(acts, grads, p_in, p_out, mask):
    ranks = p_out.shape[1] + p_in.shape[1]
    toks = acts.shape[1]
    depth = acts.shape[2] + grads.shape[2]
    return pl.pallas_call(
        project_kernel,
        out_shape=jax.ShapeDtypeStruct((ranks, toks), jnp.float32),
        in_specs=[VMEM] * 5,
        out_specs=VMEM,
        compiler_params=pltpu.CompilerParams(vmem_limit_bytes=16 << 20),
        cost_estimate=pl.CostEstimate(
            flops=toks * ranks * depth,
            bytes_accessed=2 * depth * (toks + ranks // 2),
            transcendentals=0,
        ),
    )(acts, grads, p_in, p_out, mask)


def score_kernel(blocks, rank_out, pieces, *refs):
    sides, (bounds,), queries = refs[:blocks], refs[blocks : blocks + 1], refs[blocks + 1 : -1]
    out = refs[-1]
    toks = sides[0].shape[1]
    rows = bounds.shape[0]
    rank_in = sides[0].shape[0] - rank_out
    copies = LANES // rank_in
    lane = lax.broadcasted_iota(jnp.int32, (rows, toks), 1)
    total = None
    for c in range(blocks):
        inside = (lane >= bounds[:, 2 * c : 2 * c + 1]) & (lane < bounds[:, 2 * c + 1 : 2 * c + 2])
        g = sides[c][:rank_out].astype(jnp.float32)
        a = sides[c][rank_out:]
        spread = [jnp.where(inside, g[i : i + 1], 0.0) for i in range(rank_out)]
        weighted = jnp.concatenate(spread, axis=0).astype(jnp.bfloat16)
        part = dot_last(weighted, jnp.concatenate([a] * copies, axis=0))
        total = part if total is None else total + part
    column = lax.broadcasted_iota(jnp.int32, (rows, LANES), 1) // rank_in
    flat = []
    for i in range(0, rank_out, copies):
        tile = total[i * rows : (i + 1) * rows]
        for n in range(1, copies):
            tile = jnp.where(column == n, total[(i + n) * rows : (i + n + 1) * rows], tile)
        flat.append(tile)
    sketch = jnp.concatenate(flat, axis=1).astype(jnp.bfloat16)
    core = bounds[:, 2 * blocks : 2 * blocks + 1]
    place = bounds[:, 2 * blocks + 1 : 2 * blocks + 2]
    got = [dot_last(sketch, q[0] if len(q.shape) == 3 else q[...]) for q in queries]
    groups, at = [got[0]], 1
    for _ in range(1, pieces[0]):
        parts = got[at : at + pieces[1]]
        at += pieces[1]
        ordered = []
        for n in range(pieces[1]):
            pick = parts[0]
            for h in range(1, pieces[1]):
                pick = jnp.where((core ^ h) == n, parts[h], pick)
            if pieces[1] > 1:
                pick = jnp.where(core == n, parts[0], pick)
            ordered.append(pick)
        groups.append(jnp.concatenate(ordered, axis=1))
    final = []
    for n in range(pieces[0]):
        pick = groups[0]
        for h in range(1, pieces[0]):
            pick = jnp.where((place ^ h) == n, groups[h], pick)
        final.append(pick)
    out[...] = jnp.concatenate(final, axis=1)


def scores_of(sides, bounds, queries, rank_out, pieces):
    rows = bounds.shape[0]
    width = sum(q.shape[-2] for q in queries)
    depth = queries[0].shape[-1]
    return pl.pallas_call(
        functools.partial(score_kernel, len(sides), rank_out, pieces),
        out_shape=jax.ShapeDtypeStruct((rows, width), jnp.float32),
        in_specs=[VMEM] * (len(sides) + 1 + len(queries)),
        out_specs=VMEM,
        compiler_params=pltpu.CompilerParams(vmem_limit_bytes=24 << 20),
        cost_estimate=pl.CostEstimate(
            flops=2 * rows * depth * (width + len(sides) * sides[0].shape[1]),
            bytes_accessed=2 * depth * width,
            transcendentals=0,
        ),
    )(*sides, bounds, *queries)


def local(sizes, activations, out_grads, proj_in, proj_out, queries, lengths, owner_slot, pad_mask):
    dps, layers, cores = sizes
    pair = dps // layers
    toks = activations.shape[1]
    rank_out = proj_out.shape[1]
    block = queries.shape[1]
    own_rows = lengths.shape[0] // dps
    d, l, t = lax.axis_index("dp"), lax.axis_index("layer"), lax.axis_index("tensor")
    v = d % pair

    share = block // cores
    mine = lax.dynamic_slice_in_dim(queries[0], t * share, share, 0)
    fetched = []
    for k in range(1, pair):
        fetched.append(lax.ppermute(mine, "dp", [(i, i ^ k) for i in range(dps)]))

    partial_sides = project(activations, out_grads, proj_in, proj_out, pad_mask[None])
    both = partial_sides
    for k in range(1, cores):
        both = both + lax.ppermute(partial_sides, "tensor", [(i, i ^ k) for i in range(cores)])
    sides = both.astype(jnp.bfloat16)

    grouped, left = divmod(dps - 1, cores)
    held, source, split = [sides], [d], [True]
    for j in range(grouped - 1, -1, -1):
        base = 1 + left + j * cores
        perm = [
            (i * cores + c, (i ^ (base + cores - 1 - c)) * cores + c)
            for i in range(dps)
            for c in range(cores)
        ]
        held.append(lax.ppermute(sides, ("dp", "tensor"), perm))
        source.append(d ^ (base + cores - 1 - t))
        split.append(False)
    for k in range(left, 0, -1):
        held.append(lax.ppermute(sides, "dp", [(i, i ^ k) for i in range(dps)]))
        source.append(d ^ k)
        split.append(cores > 1)

    wanted = [queries]
    for q in fetched:
        wanted.append(q)
        for k in range(1, cores):
            wanted.append(lax.ppermute(q, "tensor", [(i, i ^ k) for i in range(cores)]))

    rows = layers * own_rows
    padded = -(-rows // 8) * 8
    index = jnp.arange(padded, dtype=jnp.int32)
    slot = ((l ^ (index // own_rows)) * pair + v) * own_rows + index % own_rows
    slot = jnp.where(index < rows, slot, -1)
    ones = jnp.arange(lengths.shape[0])
    first = jnp.sum(jnp.where(ones[None, :] < ones[:, None], lengths[None, :], 0), axis=1)
    match = slot[:, None] == owner_slot[None, :]
    low = jnp.sum(jnp.where(match, first[None, :], 0), axis=1)
    size = jnp.sum(jnp.where(match, lengths[None, :], 0), axis=1)
    columns = []
    for src, cut in zip(source, split):
        start = low - src * toks
        stop = start + size
        if cut:
            start = jnp.maximum(start, t * (toks // cores))
            stop = jnp.minimum(stop, (t + 1) * (toks // cores))
        columns += [start, stop]
    columns += [jnp.full_like(low, 1) * t, jnp.full_like(low, 1) * v]
    bounds = jnp.stack(columns, axis=1)

    served = scores_of(held, bounds, wanted, rank_out, (pair, cores))

    whole = None
    for k in range(layers - 1, -1, -1):
        turn = 1 if k == 0 else 0
        perm = []
        for su in range(layers):
            for sv in range(pair):
                for sl in range(layers):
                    for c in range(cores):
                        src = ((su * pair + sv) * layers + sl) * cores + c
                        dst = ((sl ^ k) * pair + sv) * layers + su
                        perm.append((src, dst * cores + (c + turn) % cores))
        piece = served[k * own_rows : (k + 1) * own_rows]
        piece = lax.ppermute(piece, ("dp", "layer", "tensor"), perm)
        whole = piece if whole is None else whole + piece
    result = whole
    for k in range(1, cores):
        result = result + lax.ppermute(whole, "tensor", [(i, i ^ k) for i in range(cores)])
    return result


def solution(mesh):
    placed = (
        P("layer", ("groups", "dp"), "tensor"),
        P("layer", ("groups", "dp"), "tensor"),
        P("layer", None, "tensor"),
        P("layer", None, "tensor"),
        P("layer", "dp", None),
        P("groups"),
        P("groups"),
        P(("groups", "dp")),
    )
    sizes = tuple(mesh.shape[name] for name in ("dp", "layer", "tensor"))
    return jax.shard_map(
        functools.partial(local, sizes),
        mesh=mesh,
        in_specs=placed,
        out_specs=P(("groups", "dp"), "layer"),
        check_vma=False,
    )
```

```python
import functools

import jax
import jax.numpy as jnp
from jax import lax
from jax.experimental import pallas as pl
from jax.experimental.pallas import tpu as pltpu
from jax.sharding import PartitionSpec as P


VMEM = pl.BlockSpec(memory_space=pltpu.VMEM)
LANES = 128
CHUNKS = 4


def dot_last(left, right):
    return lax.dot_general(
        left, right, (((1,), (1,)), ((), ())), preferred_element_type=jnp.float32
    )


def cuts(depth, count):
    step = max(LANES, depth // count // LANES * LANES)
    edges = list(range(0, depth - step + 1, step))
    return [(lo, (edges + [depth])[n + 1] - lo) for n, lo in enumerate(edges)]


def project_kernel(acts, grads, p_in, p_out, out, acts_v, grads_v, in_v, out_v, sems):
    rank = p_out.shape[1]
    chunks = cuts(acts.shape[2], CHUNKS)
    waits = []
    for n, (lo, size) in enumerate([(0, grads.shape[2])] + chunks):
        pairs = [(grads, grads_v), (p_out, out_v)] if n == 0 else [(acts, acts_v), (p_in, in_v)]
        started = []
        for m, (src, dst) in enumerate(pairs):
            part = (slice(None), pl.ds(lo, size))
            copy = pltpu.make_async_copy(src.at[(0,) + part], dst.at[part], sems.at[2 * n + m])
            copy.start()
            started.append(copy)
        waits.append(started)
    for copy in waits[0]:
        copy.wait()
    out[:rank] = dot_last(out_v[...], grads_v[...])
    total = None
    for (lo, size), started in zip(chunks, waits[1:]):
        for copy in started:
            copy.wait()
        part = dot_last(in_v[:, pl.ds(lo, size)], acts_v[:, pl.ds(lo, size)])
        total = part if total is None else total + part
    out[rank:] = total


def project(acts, grads, p_in, p_out):
    ranks = p_out.shape[1] + p_in.shape[1]
    toks = acts.shape[1]
    depth = acts.shape[2] + grads.shape[2]
    big = [pltpu.with_memory_space_constraint(x, pltpu.HBM) for x in (acts, grads, p_in, p_out)]
    return pl.pallas_call(
        project_kernel,
        out_shape=jax.ShapeDtypeStruct((ranks, toks), jnp.float32),
        in_specs=[pl.BlockSpec(memory_space=pltpu.HBM)] * 4,
        out_specs=VMEM,
        scratch_shapes=[pltpu.VMEM(x.shape[1:], x.dtype) for x in big]
        + [pltpu.SemaphoreType.DMA((2 * len(cuts(acts.shape[2], CHUNKS)) + 2,))],
        compiler_params=pltpu.CompilerParams(vmem_limit_bytes=16 << 20),
        cost_estimate=pl.CostEstimate(
            flops=toks * ranks * depth,
            bytes_accessed=2 * depth * (toks + ranks // 2),
            transcendentals=0,
        ),
    )(*big)


def score_kernel(blocks, rank_out, pieces, *refs):
    sides, (bounds,), queries = refs[:blocks], refs[blocks : blocks + 1], refs[blocks + 1 : -1]
    out = refs[-1]
    toks = sides[0].shape[1]
    rows = bounds.shape[0]
    rank_in = sides[0].shape[0] - rank_out
    copies = LANES // rank_in
    lane = lax.broadcasted_iota(jnp.int32, (rows, toks), 1)
    total = None
    for c in range(blocks):
        inside = (lane >= bounds[:, 2 * c : 2 * c + 1]) & (lane < bounds[:, 2 * c + 1 : 2 * c + 2])
        g = sides[c][:rank_out].astype(jnp.float32)
        a = sides[c][rank_out:]
        spread = [jnp.where(inside, g[i : i + 1], 0.0) for i in range(rank_out)]
        weighted = jnp.concatenate(spread, axis=0).astype(jnp.bfloat16)
        part = dot_last(weighted, jnp.concatenate([a] * copies, axis=0))
        total = part if total is None else total + part
    column = lax.broadcasted_iota(jnp.int32, (rows, LANES), 1) // rank_in
    flat = []
    for i in range(0, rank_out, copies):
        tile = total[i * rows : (i + 1) * rows]
        for n in range(1, copies):
            tile = jnp.where(column == n, total[(i + n) * rows : (i + n + 1) * rows], tile)
        flat.append(tile)
    sketch = jnp.concatenate(flat, axis=1).astype(jnp.bfloat16)
    core = bounds[:, 2 * blocks : 2 * blocks + 1]
    place = bounds[:, 2 * blocks + 1 : 2 * blocks + 2]
    got = [dot_last(sketch, q[0] if len(q.shape) == 3 else q[...]) for q in queries]
    groups, at = [got[0]], 1
    for _ in range(1, pieces[0]):
        parts = got[at : at + pieces[1]]
        at += pieces[1]
        pick = parts[0]
        for h in range(1, pieces[1]):
            pick = jnp.where(core == (pieces[1] - 1 + h) % pieces[1], parts[h], pick)
        groups.append(pick)
    final = []
    for n in range(pieces[0]):
        pick = groups[0]
        for h in range(1, pieces[0]):
            pick = jnp.where((place ^ h) == n, groups[h], pick)
        final.append(pick)
    out[...] = jnp.concatenate(final, axis=1)


def scores_of(sides, bounds, queries, rank_out, pieces):
    rows = bounds.shape[0]
    width = pieces[0] * queries[0].shape[-2]
    depth = queries[0].shape[-1]
    return pl.pallas_call(
        functools.partial(score_kernel, len(sides), rank_out, pieces),
        out_shape=jax.ShapeDtypeStruct((rows, width), jnp.float32),
        in_specs=[VMEM] * (len(sides) + 1 + len(queries)),
        out_specs=VMEM,
        compiler_params=pltpu.CompilerParams(vmem_limit_bytes=24 << 20),
        cost_estimate=pl.CostEstimate(
            flops=2 * rows * depth * (width + len(sides) * sides[0].shape[1]),
            bytes_accessed=2 * depth * width,
            transcendentals=0,
        ),
    )(*sides, bounds, *queries)


def local(sizes, activations, out_grads, proj_in, proj_out, queries, lengths, owner_slot, pad_mask):
    dps, layers, cores = sizes
    pair = dps // layers
    toks = activations.shape[1]
    rank_out = proj_out.shape[1]
    own_rows = lengths.shape[0] // dps
    d, l, t = lax.axis_index("dp"), lax.axis_index("layer"), lax.axis_index("tensor")
    v = d % pair

    fetched = []
    for k in range(1, pair):
        perm = [
            (i * cores + c, (i if c else i ^ k) * cores + (c + cores - 1) % cores)
            for i in range(dps)
            for c in range(cores)
        ]
        fetched.append(lax.ppermute(queries[0], ("dp", "tensor"), perm))

    partial_sides = project(activations, out_grads, proj_in, proj_out)
    both = partial_sides
    for k in range(1, cores):
        both = both + lax.ppermute(partial_sides, "tensor", [(i, i ^ k) for i in range(cores)])
    is_out = lax.broadcasted_iota(jnp.int32, both.shape, 0) < rank_out
    sides = jnp.where(is_out & (pad_mask == 0)[None], 0.0, both).astype(jnp.bfloat16)

    grouped, left = divmod(dps - 1, cores)
    held, source, split = [sides], [d], [True]
    for j in range(grouped - 1, -1, -1):
        base = 1 + left + j * cores
        perm = [
            (i * cores + c, (i ^ (base + cores - 1 - c)) * cores + c)
            for i in range(dps)
            for c in range(cores)
        ]
        held.append(lax.ppermute(sides, ("dp", "tensor"), perm))
        source.append(d ^ (base + cores - 1 - t))
        split.append(False)
    for k in range(left, 0, -1):
        held.append(lax.ppermute(sides, "dp", [(i, i ^ k) for i in range(dps)]))
        source.append(d ^ k)
        split.append(cores > 1)

    wanted = [queries]
    for q in fetched:
        wanted.append(q)
        for k in range(1, cores):
            perm = [(i, (i + k) % cores) for i in range(cores)]
            wanted.append(lax.ppermute(q, "tensor", perm))

    rows = layers * own_rows
    padded = -(-rows // 8) * 8
    index = jnp.arange(padded, dtype=jnp.int32)
    slot = ((l ^ (index // own_rows)) * pair + v) * own_rows + index % own_rows
    slot = jnp.where(index < rows, slot, -1)
    ones = jnp.arange(lengths.shape[0])
    first = jnp.sum(jnp.where(ones[None, :] < ones[:, None], lengths[None, :], 0), axis=1)
    match = slot[:, None] == owner_slot[None, :]
    low = jnp.sum(jnp.where(match, first[None, :], 0), axis=1)
    size = jnp.sum(jnp.where(match, lengths[None, :], 0), axis=1)
    columns = []
    for src, cut in zip(source, split):
        start = low - src * toks
        stop = start + size
        if cut:
            start = jnp.maximum(start, t * (toks // cores))
            stop = jnp.minimum(stop, (t + 1) * (toks // cores))
        columns += [start, stop]
    columns += [jnp.full_like(low, 1) * t, jnp.full_like(low, 1) * v]
    bounds = jnp.stack(columns, axis=1)

    served = scores_of(held, bounds, wanted, rank_out, (pair, cores))

    whole = None
    for k in range(layers - 1, -1, -1):
        turn = 1 if k == 0 else 0
        perm = []
        for su in range(layers):
            for sv in range(pair):
                for sl in range(layers):
                    for c in range(cores):
                        src = ((su * pair + sv) * layers + sl) * cores + c
                        dst = ((sl ^ k) * pair + sv) * layers + su
                        perm.append((src, dst * cores + (c + turn) % cores))
        piece = served[k * own_rows : (k + 1) * own_rows]
        piece = lax.ppermute(piece, ("dp", "layer", "tensor"), perm)
        whole = piece if whole is None else whole + piece
    result = whole
    for k in range(1, cores):
        result = result + lax.ppermute(whole, "tensor", [(i, i ^ k) for i in range(cores)])
    return result


def solution(mesh):
    placed = (
        P("layer", ("groups", "dp"), "tensor"),
        P("layer", ("groups", "dp"), "tensor"),
        P("layer", None, "tensor"),
        P("layer", None, "tensor"),
        P("layer", "dp", None),
        P("groups"),
        P("groups"),
        P(("groups", "dp")),
    )
    sizes = tuple(mesh.shape[name] for name in ("dp", "layer", "tensor"))
    return jax.shard_map(
        functools.partial(local, sizes),
        mesh=mesh,
        in_specs=placed,
        out_specs=P(("groups", "dp"), "layer"),
        check_vma=False,
    )
```

```python
import functools

import jax
import jax.numpy as jnp
from jax import lax
from jax.experimental import pallas as pl
from jax.experimental.pallas import tpu as pltpu
from jax.sharding import PartitionSpec as P


VMEM = pl.BlockSpec(memory_space=pltpu.VMEM)
LANES = 128
CHUNKS = 2


def dot_last(left, right):
    return lax.dot_general(
        left, right, (((1,), (1,)), ((), ())), preferred_element_type=jnp.float32
    )


def chunk_count(depth):
    return next(n for n in (CHUNKS, 1) if depth % (n * LANES) == 0)


def project_kernel(acts, grads, p_in, p_out, out, acts_v, grads_v, in_v, out_v, sems):
    rank = p_out.shape[1]
    count = chunk_count(acts.shape[2])
    size = acts.shape[2] // count

    def copies(n):
        part = (slice(None), pl.ds(pl.multiple_of(n * size, LANES), size))
        return [
            pltpu.make_async_copy(src.at[(0,) + part], dst.at[part], sems.at[2 * n + m])
            for m, (src, dst) in enumerate([(acts, acts_v), (p_in, in_v)])
        ]

    head = [
        pltpu.make_async_copy(src.at[0], dst, sems.at[2 * count + m])
        for m, (src, dst) in enumerate([(grads, grads_v), (p_out, out_v)])
    ]
    for copy in head:
        copy.start()
    for n in range(count):
        for copy in copies(n):
            copy.start()
    for copy in head:
        copy.wait()
    out[:rank] = dot_last(out_v[...], grads_v[...])
    out[rank:] = jnp.zeros_like(out[rank:])

    def step(n, carry):
        for copy in copies(n):
            copy.wait()
        part = pl.ds(pl.multiple_of(n * size, LANES), size)
        out[rank:] += dot_last(in_v[:, part], acts_v[:, part])
        return carry

    lax.fori_loop(0, count, step, 0)


def project(acts, grads, p_in, p_out):
    ranks = p_out.shape[1] + p_in.shape[1]
    toks = acts.shape[1]
    depth = acts.shape[2] + grads.shape[2]
    big = [pltpu.with_memory_space_constraint(x, pltpu.HBM) for x in (acts, grads, p_in, p_out)]
    return pl.pallas_call(
        project_kernel,
        out_shape=jax.ShapeDtypeStruct((ranks, toks), jnp.float32),
        in_specs=[pl.BlockSpec(memory_space=pltpu.HBM)] * 4,
        out_specs=VMEM,
        scratch_shapes=[pltpu.VMEM(x.shape[1:], x.dtype) for x in big]
        + [pltpu.SemaphoreType.DMA((2 * chunk_count(acts.shape[2]) + 2,))],
        compiler_params=pltpu.CompilerParams(vmem_limit_bytes=16 << 20),
        cost_estimate=pl.CostEstimate(
            flops=toks * ranks * depth,
            bytes_accessed=2 * depth * (toks + ranks // 2),
            transcendentals=0,
        ),
    )(*big)


def score_kernel(blocks, rank_out, bounds, *refs):
    sides, queries, out = refs[:blocks], refs[blocks:-1], refs[-1]
    toks = sides[0].shape[1]
    rows = bounds.shape[0]
    rank_in = sides[0].shape[0] - rank_out
    copies = LANES // rank_in
    lane = lax.broadcasted_iota(jnp.int32, (rows, toks), 1)
    total = None
    for c in range(blocks):
        inside = (lane >= bounds[:, 2 * c : 2 * c + 1]) & (lane < bounds[:, 2 * c + 1 : 2 * c + 2])
        g = sides[c][:rank_out].astype(jnp.float32)
        a = sides[c][rank_out:]
        spread = [jnp.where(inside, g[i : i + 1], 0.0) for i in range(rank_out)]
        weighted = jnp.concatenate(spread, axis=0).astype(jnp.bfloat16)
        part = dot_last(weighted, jnp.concatenate([a] * copies, axis=0))
        total = part if total is None else total + part
    column = lax.broadcasted_iota(jnp.int32, (rows, LANES), 1) // rank_in
    flat = []
    for i in range(0, rank_out, copies):
        tile = total[i * rows : (i + 1) * rows]
        for n in range(1, copies):
            tile = jnp.where(column == n, total[(i + n) * rows : (i + n + 1) * rows], tile)
        flat.append(tile)
    sketch = jnp.concatenate(flat, axis=1).astype(jnp.bfloat16)
    place = bounds[:, 2 * blocks : 2 * blocks + 1]
    got = [dot_last(sketch, q[0] if len(q.shape) == 3 else q[...]) for q in queries]
    ordered = []
    for n in range(len(got)):
        pick = got[0]
        for k in range(1, len(got)):
            pick = jnp.where((place ^ k) == n, got[k], pick)
        ordered.append(pick)
    out[...] = jnp.concatenate(ordered, axis=1)


def scores_of(sides, bounds, queries, rank_out):
    rows = bounds.shape[0]
    width = sum(q.shape[-2] for q in queries)
    depth = queries[0].shape[-1]
    return pl.pallas_call(
        functools.partial(score_kernel, len(sides), rank_out),
        out_shape=jax.ShapeDtypeStruct((rows, width), jnp.float32),
        in_specs=[VMEM] * (len(sides) + 1 + len(queries)),
        out_specs=VMEM,
        compiler_params=pltpu.CompilerParams(vmem_limit_bytes=24 << 20),
        cost_estimate=pl.CostEstimate(
            flops=2 * rows * depth * (width + len(sides) * sides[0].shape[1]),
            bytes_accessed=2 * depth * width,
            transcendentals=0,
        ),
    )(bounds, *sides, *queries)


def to_last(dps, cores, k):
    return [
        (i * cores + c, (i if c else i ^ k) * cores + (c - 1) % cores)
        for i in range(dps)
        for c in range(cores)
    ]


def hop_order(dps):
    return [dps // 2] + [k for k in range(dps - 1, 0, -1) if k != dps // 2]


def local(sizes, activations, out_grads, proj_in, proj_out, queries, lengths, owner_slot, pad_mask):
    dps, layers, cores = sizes
    pair = dps // layers
    assert cores > 1 and dps & (dps - 1) == 0
    toks = activations.shape[1]
    rank_out = proj_out.shape[1]
    own_rows = lengths.shape[0] // dps
    d, l, t = lax.axis_index("dp"), lax.axis_index("layer"), lax.axis_index("tensor")

    v = d % pair

    wanted = [queries]
    for k in range(1, pair):
        wanted.append(lax.ppermute(queries[0], ("dp", "tensor"), to_last(dps, cores, k)))

    partial_sides = project(
        activations, out_grads, proj_in, proj_out
    )
    both = partial_sides
    for k in range(1, cores):
        both = both + lax.ppermute(partial_sides, "tensor", [(i, i ^ k) for i in range(cores)])
    is_out = lax.broadcasted_iota(jnp.int32, both.shape, 0) < rank_out
    sides = jnp.where(is_out & (pad_mask == 0)[None], 0.0, both).astype(jnp.bfloat16)

    held, source = [sides], [d]
    for k in hop_order(dps):
        held.append(lax.ppermute(sides, ("dp", "tensor"), to_last(dps, cores, k)))
        source.append(d ^ k)

    rows = layers * own_rows
    padded = -(-rows // 8) * 8
    index = jnp.arange(padded, dtype=jnp.int32)
    slot = ((l ^ (index // own_rows)) * pair + v) * own_rows + index % own_rows
    slot = jnp.where(index < rows, slot, -1)
    ones = jnp.arange(lengths.shape[0])
    first = jnp.sum(jnp.where(ones[None, :] < ones[:, None], lengths[None, :], 0), axis=1)
    match = slot[:, None] == owner_slot[None, :]
    low = jnp.sum(jnp.where(match, first[None, :], 0), axis=1)
    size = jnp.sum(jnp.where(match, lengths[None, :], 0), axis=1)
    columns = []
    for src in source:
        columns += [low - src * toks, low + size - src * toks]
    columns.append(jnp.full_like(low, 1) * v)
    bounds = jnp.stack(columns, axis=1)

    served = scores_of(held, bounds, wanted, rank_out)

    whole = None
    for k in range(layers - 1, -1, -1):
        perm = []
        for su in range(layers):
            for sv in range(pair):
                for sl in range(layers):
                    src = ((su * pair + sv) * layers + sl) * cores
                    dst = (((sl ^ k) * pair + sv) * layers + su) * cores
                    perm.append((src + cores - 1, dst))
                    perm += [(src + c, src + c + 1) for c in range(cores - 1)]
        piece = served[k * own_rows : (k + 1) * own_rows]
        piece = lax.ppermute(piece, ("dp", "layer", "tensor"), perm)
        whole = piece if whole is None else whole + piece
    result = whole
    for k in range(1, cores):
        other = lax.ppermute(whole, "tensor", [(i, i ^ k) for i in range(cores)])
        result = jnp.where(t == k, other, result)
    return result


def solution(mesh):
    placed = (
        P("layer", ("groups", "dp"), "tensor"),
        P("layer", ("groups", "dp"), "tensor"),
        P("layer", None, "tensor"),
        P("layer", None, "tensor"),
        P("layer", "dp", None),
        P("groups"),
        P("groups"),
        P(("groups", "dp")),
    )
    sizes = tuple(mesh.shape[name] for name in ("dp", "layer", "tensor"))
    return jax.shard_map(
        functools.partial(local, sizes),
        mesh=mesh,
        in_specs=placed,
        out_specs=P(("groups", "dp"), "layer"),
        check_vma=False,
    )
```

```python
import functools

import jax
import jax.numpy as jnp
from jax import lax
from jax.experimental import pallas as pl
from jax.experimental.pallas import tpu as pltpu
from jax.sharding import PartitionSpec as P


VMEM = pl.BlockSpec(memory_space=pltpu.VMEM)
LANES = 128
CHUNKS = 2


def dot_last(left, right):
    return lax.dot_general(
        left, right, (((1,), (1,)), ((), ())), preferred_element_type=jnp.float32
    )


def chunk_count(depth):
    return next(n for n in (CHUNKS, 1) if depth % (n * LANES) == 0)


def project_kernel(acts, grads, p_in, p_out, out, acts_v, grads_v, in_v, out_v, sems):
    rank = p_out.shape[1]
    count = chunk_count(acts.shape[2])
    size = acts.shape[2] // count

    def copies(n):
        part = (slice(None), pl.ds(pl.multiple_of(n * size, LANES), size))
        return [
            pltpu.make_async_copy(src.at[(0,) + part], dst.at[part], sems.at[2 * n + m])
            for m, (src, dst) in enumerate([(acts, acts_v), (p_in, in_v)])
        ]

    head = [
        pltpu.make_async_copy(src.at[0], dst, sems.at[2 * count + m])
        for m, (src, dst) in enumerate([(grads, grads_v), (p_out, out_v)])
    ]
    for copy in head:
        copy.start()
    for n in range(count):
        for copy in copies(n):
            copy.start()
    for copy in head:
        copy.wait()
    out[:rank] = dot_last(out_v[...], grads_v[...])
    out[rank:] = jnp.zeros_like(out[rank:])

    def step(n, carry):
        for copy in copies(n):
            copy.wait()
        part = pl.ds(pl.multiple_of(n * size, LANES), size)
        out[rank:] += dot_last(in_v[:, part], acts_v[:, part])
        return carry

    lax.fori_loop(0, count, step, 0)


def project(acts, grads, p_in, p_out):
    ranks = p_out.shape[1] + p_in.shape[1]
    toks = acts.shape[1]
    depth = acts.shape[2] + grads.shape[2]
    big = [pltpu.with_memory_space_constraint(x, pltpu.HBM) for x in (acts, grads, p_in, p_out)]
    return pl.pallas_call(
        project_kernel,
        out_shape=jax.ShapeDtypeStruct((ranks, toks), jnp.float32),
        in_specs=[pl.BlockSpec(memory_space=pltpu.HBM)] * 4,
        out_specs=VMEM,
        scratch_shapes=[pltpu.VMEM(x.shape[1:], x.dtype) for x in big]
        + [pltpu.SemaphoreType.DMA((2 * chunk_count(acts.shape[2]) + 2,))],
        compiler_params=pltpu.CompilerParams(vmem_limit_bytes=16 << 20),
        cost_estimate=pl.CostEstimate(
            flops=toks * ranks * depth,
            bytes_accessed=2 * depth * (toks + ranks // 2),
            transcendentals=0,
        ),
    )(*big)


def gather_kernel(first, count, scored, rank_out, *refs):
    refs = list(refs)
    bounds = refs.pop(0)
    before = None if first == 0 else refs.pop(0)
    sides, queries, out = refs[:count], refs[count:-1], refs[-1]
    toks = sides[0].shape[1]
    rows = bounds.shape[0]
    rank_in = sides[0].shape[0] - rank_out
    copies = LANES // rank_in
    lane = lax.broadcasted_iota(jnp.int32, (rows, toks), 1)
    total = None if before is None else before[...]
    for c in range(count):
        low, high = 2 * (first + c), 2 * (first + c) + 1
        inside = (lane >= bounds[:, low : low + 1]) & (lane < bounds[:, high : high + 1])
        g = sides[c][:rank_out].astype(jnp.float32)
        a = sides[c][rank_out:]
        spread = [jnp.where(inside, g[i : i + 1], 0.0) for i in range(rank_out)]
        weighted = jnp.concatenate(spread, axis=0).astype(jnp.bfloat16)
        part = dot_last(weighted, jnp.concatenate([a] * copies, axis=0))
        total = part if total is None else total + part
    if not scored:
        out[...] = total
        return
    column = lax.broadcasted_iota(jnp.int32, (rows, LANES), 1) // rank_in
    flat = []
    for i in range(0, rank_out, copies):
        tile = total[i * rows : (i + 1) * rows]
        for n in range(1, copies):
            tile = jnp.where(column == n, total[(i + n) * rows : (i + n + 1) * rows], tile)
        flat.append(tile)
    sketch = jnp.concatenate(flat, axis=1).astype(jnp.bfloat16)
    place = bounds[:, bounds.shape[1] - 1 :]
    got = [dot_last(sketch, q[0] if len(q.shape) == 3 else q[...]) for q in queries]
    ordered = []
    for n in range(len(got)):
        pick = got[0]
        for k in range(1, len(got)):
            pick = jnp.where((place ^ k) == n, got[k], pick)
        ordered.append(pick)
    out[...] = jnp.concatenate(ordered, axis=1)


def gather(bounds, before, first, sides, queries, rank_out):
    rows = bounds.shape[0]
    args = [bounds] + ([] if before is None else [before]) + list(sides) + list(queries)
    width = sum(q.shape[-2] for q in queries)
    depth = queries[0].shape[-1] if queries else 0
    shape = (rows, width) if queries else (rows * rank_out, LANES)
    return pl.pallas_call(
        functools.partial(gather_kernel, first, len(sides), bool(queries), rank_out),
        out_shape=jax.ShapeDtypeStruct(shape, jnp.float32),
        in_specs=[VMEM] * len(args),
        out_specs=VMEM,
        compiler_params=pltpu.CompilerParams(vmem_limit_bytes=24 << 20),
        cost_estimate=pl.CostEstimate(
            flops=2 * rows * (depth * width + rank_out * LANES * len(sides) * sides[0].shape[1]),
            bytes_accessed=2 * depth * width + rows * rank_out * LANES * 4,
            transcendentals=0,
        ),
    )(*args)


def scores_of(sides, bounds, queries, rank_out):
    total = None
    for first, last in [(n, n + 1) for n in range(len(sides))]:
        asked = queries if last == len(sides) else []
        total = gather(bounds, total, first, sides[first:last], asked, rank_out)
    return total


def to_last(dps, cores, k):
    return [
        (i * cores + c, (i if c else i ^ k) * cores + (c - 1) % cores)
        for i in range(dps)
        for c in range(cores)
    ]


def hop_order(dps):
    return list(range(dps - 1, 0, -1))


def local(sizes, activations, out_grads, proj_in, proj_out, queries, lengths, owner_slot, pad_mask):
    dps, layers, cores = sizes
    pair = dps // layers
    assert cores > 1 and dps & (dps - 1) == 0
    toks = activations.shape[1]
    rank_out = proj_out.shape[1]
    own_rows = lengths.shape[0] // dps
    d, l, t = lax.axis_index("dp"), lax.axis_index("layer"), lax.axis_index("tensor")

    v = d % pair

    wanted = [queries]
    for k in range(1, pair):
        wanted.append(lax.ppermute(queries[0], ("dp", "tensor"), to_last(dps, cores, k)))

    partial_sides = project(
        activations, out_grads, proj_in, proj_out
    )
    both = partial_sides
    for k in range(1, cores):
        both = both + lax.ppermute(partial_sides, "tensor", [(i, i ^ k) for i in range(cores)])
    is_out = lax.broadcasted_iota(jnp.int32, both.shape, 0) < rank_out
    sides = jnp.where(is_out & (pad_mask == 0)[None], 0.0, both).astype(jnp.bfloat16)

    held, source = [sides], [d]
    for k in hop_order(dps):
        held.append(lax.ppermute(sides, ("dp", "tensor"), to_last(dps, cores, k)))
        source.append(d ^ k)

    rows = layers * own_rows
    padded = -(-rows // 8) * 8
    index = jnp.arange(padded, dtype=jnp.int32)
    slot = ((l ^ (index // own_rows)) * pair + v) * own_rows + index % own_rows
    slot = jnp.where(index < rows, slot, -1)
    ones = jnp.arange(lengths.shape[0])
    first = jnp.sum(jnp.where(ones[None, :] < ones[:, None], lengths[None, :], 0), axis=1)
    match = slot[:, None] == owner_slot[None, :]
    low = jnp.sum(jnp.where(match, first[None, :], 0), axis=1)
    size = jnp.sum(jnp.where(match, lengths[None, :], 0), axis=1)
    columns = []
    for src in source:
        columns += [low - src * toks, low + size - src * toks]
    columns.append(jnp.full_like(low, 1) * v)
    bounds = jnp.stack(columns, axis=1)

    served = scores_of(held, bounds, wanted, rank_out)

    whole = None
    for k in range(layers):
        perm = []
        for su in range(layers):
            for sv in range(pair):
                for sl in range(layers):
                    src = ((su * pair + sv) * layers + sl) * cores
                    dst = (((sl ^ k) * pair + sv) * layers + su) * cores
                    perm.append((src + cores - 1, dst))
                    perm += [(src + c, src + c + 1) for c in range(cores - 1)]
        piece = served[k * own_rows : (k + 1) * own_rows]
        piece = lax.ppermute(piece, ("dp", "layer", "tensor"), perm)
        whole = piece if whole is None else whole + piece
    result = whole
    for k in range(1, cores):
        other = lax.ppermute(whole, "tensor", [(i, i ^ k) for i in range(cores)])
        result = jnp.where(t == k, other, result)
    return result


def solution(mesh):
    placed = (
        P("layer", ("groups", "dp"), "tensor"),
        P("layer", ("groups", "dp"), "tensor"),
        P("layer", None, "tensor"),
        P("layer", None, "tensor"),
        P("layer", "dp", None),
        P("groups"),
        P("groups"),
        P(("groups", "dp")),
    )
    sizes = tuple(mesh.shape[name] for name in ("dp", "layer", "tensor"))
    return jax.shard_map(
        functools.partial(local, sizes),
        mesh=mesh,
        in_specs=placed,
        out_specs=P(("groups", "dp"), "layer"),
        check_vma=False,
    )
```

```python
import functools

import jax
import jax.numpy as jnp
from jax import lax
from jax.experimental import pallas as pl
from jax.experimental.pallas import tpu as pltpu
from jax.sharding import PartitionSpec as P


VMEM = pl.BlockSpec(memory_space=pltpu.VMEM)
LANES = 128
CHUNKS = 2


def dot_last(left, right):
    return lax.dot_general(
        left, right, (((1,), (1,)), ((), ())), preferred_element_type=jnp.float32
    )


def chunk_count(depth):
    return next(n for n in (CHUNKS, 1) if depth % (n * LANES) == 0)


def project_kernel(acts, grads, p_in, p_out, out, acts_v, grads_v, in_v, out_v, sems):
    rank = p_out.shape[1]
    count = chunk_count(acts.shape[2])
    size = acts.shape[2] // count

    def copies(n):
        part = (slice(None), pl.ds(pl.multiple_of(n * size, LANES), size))
        return [
            pltpu.make_async_copy(src.at[(0,) + part], dst.at[part], sems.at[2 * n + m])
            for m, (src, dst) in enumerate([(acts, acts_v), (p_in, in_v)])
        ]

    head = [
        pltpu.make_async_copy(src.at[0], dst, sems.at[2 * count + m])
        for m, (src, dst) in enumerate([(grads, grads_v), (p_out, out_v)])
    ]
    for copy in head:
        copy.start()
    for n in range(count):
        for copy in copies(n):
            copy.start()
    for copy in head:
        copy.wait()
    out[:rank] = dot_last(out_v[...], grads_v[...])
    out[rank:] = jnp.zeros_like(out[rank:])

    def step(n, carry):
        for copy in copies(n):
            copy.wait()
        part = pl.ds(pl.multiple_of(n * size, LANES), size)
        out[rank:] += dot_last(in_v[:, part], acts_v[:, part])
        return carry

    lax.fori_loop(0, count, step, 0)


def project(acts, grads, p_in, p_out):
    ranks = p_out.shape[1] + p_in.shape[1]
    toks = acts.shape[1]
    depth = acts.shape[2] + grads.shape[2]
    big = [pltpu.with_memory_space_constraint(x, pltpu.HBM) for x in (acts, grads, p_in, p_out)]
    return pl.pallas_call(
        project_kernel,
        out_shape=jax.ShapeDtypeStruct((ranks, toks), jnp.float32),
        in_specs=[pl.BlockSpec(memory_space=pltpu.HBM)] * 4,
        out_specs=VMEM,
        scratch_shapes=[pltpu.VMEM(x.shape[1:], x.dtype) for x in big]
        + [pltpu.SemaphoreType.DMA((2 * chunk_count(acts.shape[2]) + 2,))],
        compiler_params=pltpu.CompilerParams(vmem_limit_bytes=16 << 20),
        cost_estimate=pl.CostEstimate(
            flops=toks * ranks * depth,
            bytes_accessed=2 * depth * (toks + ranks // 2),
            transcendentals=0,
        ),
    )(*big)


def sketch_kernel(cores, rank_out, bounds, mask, *refs):
    shares, outs = refs[:cores], refs[cores:]
    rows, toks = bounds.shape[0], mask.shape[1]
    rank_in = shares[0].shape[0] - rank_out
    copies = LANES // rank_in
    lane = lax.broadcasted_iota(jnp.int32, (rows, toks), 1)
    inside = (lane >= bounds[:, 0:1]) & (lane < bounds[:, 1:2]) & (mask[...] != 0)
    both = shares[0][...]
    for share in shares[1:]:
        both = both + share[...]
    both = both.astype(jnp.bfloat16)
    g, a = both[:rank_out].astype(jnp.float32), both[rank_out:]
    spread = [jnp.where(inside, g[i : i + 1], 0.0) for i in range(rank_out)]
    weighted = jnp.concatenate(spread, axis=0).astype(jnp.bfloat16)
    total = dot_last(weighted, jnp.concatenate([a] * copies, axis=0))
    column = lax.broadcasted_iota(jnp.int32, (rows, LANES), 1) // rank_in
    flat = []
    for i in range(0, rank_out, copies):
        tile = total[i * rows : (i + 1) * rows]
        for n in range(1, copies):
            tile = jnp.where(column == n, total[(i + n) * rows : (i + n + 1) * rows], tile)
        flat.append(tile)
    sketch = jnp.concatenate(flat, axis=1)
    part = rows // len(outs)
    for n, out in enumerate(outs):
        out[...] = sketch[n * part : (n + 1) * part].astype(out.dtype)


def sketches_of(shares, bounds, mask, rank_out, pair):
    rows = bounds.shape[0]
    depth = rank_out * (shares[0].shape[0] - rank_out)
    return pl.pallas_call(
        functools.partial(sketch_kernel, len(shares), rank_out),
        out_shape=[jax.ShapeDtypeStruct((rows // pair, depth), jnp.bfloat16)] * pair,
        in_specs=[VMEM] * (len(shares) + 2),
        out_specs=[VMEM] * pair,
        compiler_params=pltpu.CompilerParams(vmem_limit_bytes=24 << 20),
        cost_estimate=pl.CostEstimate(
            flops=2 * rows * depth * mask.shape[1],
            bytes_accessed=2 * rows * depth,
            transcendentals=0,
        ),
    )(bounds, mask, *shares)


def score_kernel(count, bounds, *refs):
    sketches, queries, out = refs[:count], refs[count:-1], refs[-1]
    total = sketches[0][...].astype(jnp.float32)
    for sketch in sketches[1:]:
        total = total + sketch[...].astype(jnp.float32)
    total = total.astype(jnp.bfloat16)
    rows = total.shape[0]
    place = bounds[:rows, 2:3]
    got = [dot_last(total, q[0] if len(q.shape) == 3 else q[...]) for q in queries]
    ordered = []
    for n in range(len(got)):
        pick = got[0]
        for k in range(1, len(got)):
            pick = jnp.where((place ^ k) == n, got[k], pick)
        ordered.append(pick)
    out[...] = jnp.concatenate(ordered, axis=1)


def scores_of(sketches, bounds, queries):
    rows, depth = sketches[0].shape
    width = sum(q.shape[-2] for q in queries)
    return pl.pallas_call(
        functools.partial(score_kernel, len(sketches)),
        out_shape=jax.ShapeDtypeStruct((rows, width), jnp.float32),
        in_specs=[VMEM] * (1 + len(sketches) + len(queries)),
        out_specs=VMEM,
        compiler_params=pltpu.CompilerParams(vmem_limit_bytes=24 << 20),
        cost_estimate=pl.CostEstimate(
            flops=2 * rows * depth * width, bytes_accessed=2 * depth * width, transcendentals=0
        ),
    )(bounds, *sketches, *queries)


def to_last(dps, cores, k):
    return [
        (i * cores + c, (i if c else i ^ k) * cores + (c - 1) % cores)
        for i in range(dps)
        for c in range(cores)
    ]


def home_perm(sizes, k):
    dps, layers, cores = sizes
    pair = dps // layers
    perm = []
    for u in range(layers):
        for v in range(pair):
            for l in range(layers):
                src = ((u * pair + v) * layers + l) * cores
                dst = (((l ^ k) * pair + v) * layers + u) * cores
                side = ((u * pair + v) * layers + (l ^ 1)) * cores
                chain = [(src + c, src + c + 1) for c in range(cores - 1)]
                if k or layers != 2:
                    perm += [(src + cores - 1, dst)] + chain
                elif u != l:
                    perm += [(src + cores - 1, dst), (src, side)]
                    perm += [(src + c, src + c + 1) for c in range(1, cores - 1)]
                else:
                    perm += [(src + cores - 1, side + 1)] + chain
    return perm


def hop_order(dps):
    return [1] + list(range(dps - 1, 1, -1))


def local(sizes, activations, out_grads, proj_in, proj_out, queries, lengths, owner_slot, pad_mask):
    dps, layers, cores = sizes
    pair = dps // layers
    assert cores > 1 and dps & (dps - 1) == 0
    toks = activations.shape[1]
    rank_out = proj_out.shape[1]
    own_rows = lengths.shape[0] // dps
    d, l, t = lax.axis_index("dp"), lax.axis_index("layer"), lax.axis_index("tensor")

    v = d % pair

    wanted = [queries]
    for k in range(1, pair):
        wanted.append(lax.ppermute(queries[0], ("dp", "tensor"), to_last(dps, cores, k)))

    partial_sides = project(
        activations, out_grads, proj_in, proj_out
    )
    shares = [partial_sides]
    for k in range(1, cores):
        shares.append(lax.ppermute(partial_sides, "tensor", [(i, i ^ k) for i in range(cores)]))

    rows = layers * own_rows
    index = jnp.arange(pair * rows, dtype=jnp.int32)
    turn = index // rows
    half = l ^ (index % rows // own_rows)
    slot = (half * pair + (v ^ turn)) * own_rows + index % own_rows
    count = jnp.arange(lengths.shape[0])
    first = jnp.sum(jnp.where(count[None, :] < count[:, None], lengths[None, :], 0), axis=1)
    match = slot[:, None] == owner_slot[None, :]
    low = jnp.sum(jnp.where(match, first[None, :], 0), axis=1) - d * toks
    high = low + jnp.sum(jnp.where(match, lengths[None, :], 0), axis=1)
    column = jnp.arange(3)[None, :]
    bounds = jnp.where(column == 0, low[:, None], jnp.where(column == 1, high[:, None], v))

    sketches = sketches_of(shares, bounds, pad_mask[None], rank_out, pair)

    held = [sketches[0]]
    for k in hop_order(dps):
        held.append(lax.ppermute(sketches[k % pair], ("dp", "tensor"), to_last(dps, cores, k)))

    served = scores_of(held, bounds, wanted)

    whole = None
    for k in range(layers):
        perm = home_perm(sizes, k)
        piece = served[k * own_rows : (k + 1) * own_rows]
        piece = lax.ppermute(piece, ("dp", "layer", "tensor"), perm)
        if k == 0 and layers == 2:
            piece = jnp.where(d // pair == l, 0.0, piece)
        whole = piece if whole is None else whole + piece
    if layers == 2:
        kept = jnp.where(d // pair == l, served[:own_rows], 0.0)
    else:
        kept = jnp.zeros_like(whole)
    parts = jnp.where(t == 0, whole, jnp.where(t == cores - 1, kept, 0.0))
    result = parts
    for k in range(1, cores):
        result = result + lax.ppermute(
            parts, "tensor", [(i, i ^ k) for i in range(cores)]
        )
    return result


def solution(mesh):
    placed = (
        P("layer", ("groups", "dp"), "tensor"),
        P("layer", ("groups", "dp"), "tensor"),
        P("layer", None, "tensor"),
        P("layer", None, "tensor"),
        P("layer", "dp", None),
        P("groups"),
        P("groups"),
        P(("groups", "dp")),
    )
    sizes = tuple(mesh.shape[name] for name in ("dp", "layer", "tensor"))
    return jax.shard_map(
        functools.partial(local, sizes),
        mesh=mesh,
        in_specs=placed,
        out_specs=P(("groups", "dp"), "layer"),
        check_vma=False,
    )
```

```python
import functools

import jax
import jax.numpy as jnp
from jax import lax
from jax.experimental import pallas as pl
from jax.experimental.pallas import tpu as pltpu
from jax.sharding import PartitionSpec as P


VMEM = pl.BlockSpec(memory_space=pltpu.VMEM)
LANES = 128
CHUNKS = 2


def dot_last(left, right):
    return lax.dot_general(
        left, right, (((1,), (1,)), ((), ())), preferred_element_type=jnp.float32
    )


def chunk_count(depth):
    return next(n for n in (CHUNKS, 1) if depth % (n * LANES) == 0)


def project_kernel(acts, grads, p_in, p_out, out, sent, acts_v, grads_v, in_v, out_v, sems):
    rank = p_out.shape[1]
    count = chunk_count(acts.shape[2])
    size = acts.shape[2] // count

    def copies(n):
        part = (slice(None), pl.ds(pl.multiple_of(n * size, LANES), size))
        return [
            pltpu.make_async_copy(src.at[(0,) + part], dst.at[part], sems.at[2 * n + m])
            for m, (src, dst) in enumerate([(acts, acts_v), (p_in, in_v)])
        ]

    head = [
        pltpu.make_async_copy(src.at[0], dst, sems.at[2 * count + m])
        for m, (src, dst) in enumerate([(grads, grads_v), (p_out, out_v)])
    ]
    for copy in head:
        copy.start()
    for n in range(count):
        for copy in copies(n):
            copy.start()
    for copy in head:
        copy.wait()
    out[:rank] = dot_last(out_v[...], grads_v[...])
    out[rank:] = jnp.zeros_like(out[rank:])

    def step(n, carry):
        for copy in copies(n):
            copy.wait()
        part = pl.ds(pl.multiple_of(n * size, LANES), size)
        out[rank:] += dot_last(in_v[:, part], acts_v[:, part])
        return carry

    lax.fori_loop(0, count, step, 0)
    sent[...] = out[...].astype(sent.dtype)


def project(acts, grads, p_in, p_out):
    ranks = p_out.shape[1] + p_in.shape[1]
    toks = acts.shape[1]
    depth = acts.shape[2] + grads.shape[2]
    big = [pltpu.with_memory_space_constraint(x, pltpu.HBM) for x in (acts, grads, p_in, p_out)]
    return pl.pallas_call(
        project_kernel,
        out_shape=[jax.ShapeDtypeStruct((ranks, toks), x) for x in (jnp.float32, jnp.bfloat16)],
        in_specs=[pl.BlockSpec(memory_space=pltpu.HBM)] * 4,
        out_specs=[VMEM] * 2,
        scratch_shapes=[pltpu.VMEM(x.shape[1:], x.dtype) for x in big]
        + [pltpu.SemaphoreType.DMA((2 * chunk_count(acts.shape[2]) + 2,))],
        compiler_params=pltpu.CompilerParams(vmem_limit_bytes=16 << 20),
        cost_estimate=pl.CostEstimate(
            flops=toks * ranks * depth,
            bytes_accessed=2 * depth * (toks + ranks // 2),
            transcendentals=0,
        ),
    )(*big)


def sketch_kernel(cores, rank_out, bounds, mask, *refs):
    shares, outs = refs[:cores], refs[cores:]
    rows, toks = bounds.shape[0], mask.shape[1]
    rank_in = shares[0].shape[0] - rank_out
    copies = LANES // rank_in
    lane = lax.broadcasted_iota(jnp.int32, (rows, toks), 1)
    inside = (lane >= bounds[:, 0:1]) & (lane < bounds[:, 1:2]) & (mask[...] != 0)
    both = shares[0][...]
    for share in shares[1:]:
        both = both + share[...].astype(jnp.float32)
    both = both.astype(jnp.bfloat16)
    g, a = both[:rank_out].astype(jnp.float32), both[rank_out:]
    spread = [jnp.where(inside, g[i : i + 1], 0.0) for i in range(rank_out)]
    weighted = jnp.concatenate(spread, axis=0).astype(jnp.bfloat16)
    total = dot_last(weighted, jnp.concatenate([a] * copies, axis=0))
    column = lax.broadcasted_iota(jnp.int32, (rows, LANES), 1) // rank_in
    flat = []
    for i in range(0, rank_out, copies):
        tile = total[i * rows : (i + 1) * rows]
        for n in range(1, copies):
            tile = jnp.where(column == n, total[(i + n) * rows : (i + n + 1) * rows], tile)
        flat.append(tile)
    sketch = jnp.concatenate(flat, axis=1)
    part = rows // len(outs)
    for n, out in enumerate(outs):
        out[...] = sketch[n * part : (n + 1) * part].astype(out.dtype)


def sketches_of(shares, bounds, mask, rank_out, pair):
    rows = bounds.shape[0]
    depth = rank_out * (shares[0].shape[0] - rank_out)
    return pl.pallas_call(
        functools.partial(sketch_kernel, len(shares), rank_out),
        out_shape=[jax.ShapeDtypeStruct((rows // pair, depth), jnp.bfloat16)] * pair,
        in_specs=[VMEM] * (len(shares) + 2),
        out_specs=[VMEM] * pair,
        compiler_params=pltpu.CompilerParams(vmem_limit_bytes=24 << 20),
        cost_estimate=pl.CostEstimate(
            flops=2 * rows * depth * mask.shape[1],
            bytes_accessed=2 * rows * depth,
            transcendentals=0,
        ),
    )(bounds, mask, *shares)


def score_kernel(count, worker, bounds, *refs):
    sketches, queries, out = refs[:count], refs[count:-1], refs[-1]
    out[...] = jnp.zeros_like(out)

    @pl.when(lax.axis_index("tensor") == worker)
    def _():
        total = sketches[0][...].astype(jnp.float32)
        for sketch in sketches[1:]:
            total = total + sketch[...].astype(jnp.float32)
        total = total.astype(jnp.bfloat16)
        place = bounds[: total.shape[0], 2:3]
        got = [dot_last(total, q[0] if len(q.shape) == 3 else q[...]) for q in queries]
        ordered = []
        for n in range(len(got)):
            pick = got[0]
            for k in range(1, len(got)):
                pick = jnp.where((place ^ k) == n, got[k], pick)
            ordered.append(pick)
        out[...] = jnp.concatenate(ordered, axis=1)


def scores_of(sketches, bounds, queries, worker):
    rows, depth = sketches[0].shape
    width = sum(q.shape[-2] for q in queries)
    return pl.pallas_call(
        functools.partial(score_kernel, len(sketches), worker),
        out_shape=jax.ShapeDtypeStruct((rows, width), jnp.float32),
        in_specs=[VMEM] * (1 + len(sketches) + len(queries)),
        out_specs=VMEM,
        compiler_params=pltpu.CompilerParams(vmem_limit_bytes=24 << 20),
        cost_estimate=pl.CostEstimate(
            flops=2 * rows * depth * width, bytes_accessed=2 * depth * width, transcendentals=0
        ),
    )(bounds, *sketches, *queries)


def to_last(dps, cores, k):
    return [
        (i * cores + c, (i if c else i ^ k) * cores + (c - 1) % cores)
        for i in range(dps)
        for c in range(cores)
    ]


def home_perm(sizes, k):
    dps, layers, cores = sizes
    pair = dps // layers
    perm = []
    for u in range(layers):
        for v in range(pair):
            for l in range(layers):
                src = ((u * pair + v) * layers + l) * cores
                dst = (((l ^ k) * pair + v) * layers + u) * cores
                side = ((u * pair + v) * layers + (l ^ 1)) * cores
                chain = [(src + c, src + c + 1) for c in range(cores - 1)]
                if k or layers != 2:
                    perm += [(src + cores - 1, dst)] + chain
                elif u != l:
                    perm += [(src + cores - 1, dst), (src, side)]
                    perm += [(src + c, src + c + 1) for c in range(1, cores - 1)]
                else:
                    perm += [(src + cores - 1, side + 1)] + chain
    return perm


def hop_order(dps):
    return [1] + list(range(dps - 1, 1, -1))


def local(sizes, activations, out_grads, proj_in, proj_out, queries, lengths, owner_slot, pad_mask):
    dps, layers, cores = sizes
    pair = dps // layers
    assert cores > 1 and dps & (dps - 1) == 0
    toks = activations.shape[1]
    rank_out = proj_out.shape[1]
    own_rows = lengths.shape[0] // dps
    d, l, t = lax.axis_index("dp"), lax.axis_index("layer"), lax.axis_index("tensor")

    v = d % pair

    wanted = [queries]
    for k in range(1, pair):
        wanted.append(lax.ppermute(queries[0], ("dp", "tensor"), to_last(dps, cores, k)))

    partial_sides, sent_sides = project(
        activations, out_grads, proj_in, proj_out
    )
    shares = [partial_sides]
    for k in range(1, cores):
        shares.append(lax.ppermute(sent_sides, "tensor", [(i, i ^ k) for i in range(cores)]))

    rows = layers * own_rows
    index = jnp.arange(pair * rows, dtype=jnp.int32)
    turn = index // rows
    half = l ^ (index % rows // own_rows)
    slot = (half * pair + (v + turn) % pair) * own_rows + index % own_rows
    count = jnp.arange(lengths.shape[0])
    first = jnp.sum(jnp.where(count[None, :] < count[:, None], lengths[None, :], 0), axis=1)
    match = slot[:, None] == owner_slot[None, :]
    low = jnp.sum(jnp.where(match, first[None, :], 0), axis=1) - d * toks
    high = low + jnp.sum(jnp.where(match, lengths[None, :], 0), axis=1)
    column = jnp.arange(3)[None, :]
    bounds = jnp.where(column == 0, low[:, None], jnp.where(column == 1, high[:, None], v))

    sketches = sketches_of(shares, bounds, pad_mask[None], rank_out, pair)

    held = [sketches[0]]
    for k in hop_order(dps):
        perm = [
            (i * cores + c, (i if c else (i + k) % dps) * cores + (c - 1) % cores)
            for i in range(dps)
            for c in range(cores)
        ]
        held.append(lax.ppermute(sketches[k % pair], ("dp", "tensor"), perm))

    served = scores_of(held, bounds, wanted, cores - 1)

    whole = None
    for k in range(layers):
        perm = home_perm(sizes, k)
        piece = served[k * own_rows : (k + 1) * own_rows]
        piece = lax.ppermute(piece, ("dp", "layer", "tensor"), perm)
        if k == 0 and layers == 2:
            piece = jnp.where(d // pair == l, 0.0, piece)
        whole = piece if whole is None else whole + piece
    if layers == 2:
        kept = jnp.where(d // pair == l, served[:own_rows], 0.0)
    else:
        kept = jnp.zeros_like(whole)
    parts = jnp.where(t == 0, whole, jnp.where(t == cores - 1, kept, 0.0))
    result = parts
    for k in range(1, cores):
        result = result + lax.ppermute(
            parts, "tensor", [(i, i ^ k) for i in range(cores)]
        )
    return result


def solution(mesh):
    placed = (
        P("layer", ("groups", "dp"), "tensor"),
        P("layer", ("groups", "dp"), "tensor"),
        P("layer", None, "tensor"),
        P("layer", None, "tensor"),
        P("layer", "dp", None),
        P("groups"),
        P("groups"),
        P(("groups", "dp")),
    )
    sizes = tuple(mesh.shape[name] for name in ("dp", "layer", "tensor"))
    return jax.shard_map(
        functools.partial(local, sizes),
        mesh=mesh,
        in_specs=placed,
        out_specs=P(("groups", "dp"), "layer"),
        check_vma=False,
    )
```

```python
import functools

import jax
import jax.numpy as jnp
from jax import lax
from jax.experimental import pallas as pl
from jax.experimental.pallas import tpu as pltpu
from jax.sharding import PartitionSpec as P


VMEM = pl.BlockSpec(memory_space=pltpu.VMEM)
LANES = 128
CHUNKS = 2


def dot_last(left, right):
    return lax.dot_general(
        left, right, (((1,), (1,)), ((), ())), preferred_element_type=jnp.float32
    )


def chunk_count(depth):
    return next(n for n in (CHUNKS, 1) if depth % (n * LANES) == 0)


def project_kernel(acts, grads, p_in, p_out, out, acts_v, grads_v, in_v, out_v, sems):
    rank = p_out.shape[1]
    count = chunk_count(acts.shape[2])
    size = acts.shape[2] // count

    def copies(n):
        part = (slice(None), pl.ds(pl.multiple_of(n * size, LANES), size))
        return [
            pltpu.make_async_copy(src.at[(0,) + part], dst.at[part], sems.at[2 * n + m])
            for m, (src, dst) in enumerate([(acts, acts_v), (p_in, in_v)])
        ]

    head = [
        pltpu.make_async_copy(src.at[0], dst, sems.at[2 * count + m])
        for m, (src, dst) in enumerate([(grads, grads_v), (p_out, out_v)])
    ]
    for copy in head:
        copy.start()
    for n in range(count):
        for copy in copies(n):
            copy.start()
    for copy in head:
        copy.wait()
    out[:rank] = dot_last(out_v[...], grads_v[...])
    out[rank:] = jnp.zeros_like(out[rank:])

    def step(n, carry):
        for copy in copies(n):
            copy.wait()
        part = pl.ds(pl.multiple_of(n * size, LANES), size)
        out[rank:] += dot_last(in_v[:, part], acts_v[:, part])
        return carry

    lax.fori_loop(0, count, step, 0)


def project(acts, grads, p_in, p_out):
    ranks = p_out.shape[1] + p_in.shape[1]
    toks = acts.shape[1]
    depth = acts.shape[2] + grads.shape[2]
    big = [pltpu.with_memory_space_constraint(x, pltpu.HBM) for x in (acts, grads, p_in, p_out)]
    return pl.pallas_call(
        project_kernel,
        out_shape=jax.ShapeDtypeStruct((ranks, toks), jnp.float32),
        in_specs=[pl.BlockSpec(memory_space=pltpu.HBM)] * 4,
        out_specs=VMEM,
        scratch_shapes=[pltpu.VMEM(x.shape[1:], x.dtype) for x in big]
        + [pltpu.SemaphoreType.DMA((2 * chunk_count(acts.shape[2]) + 2,))],
        compiler_params=pltpu.CompilerParams(vmem_limit_bytes=16 << 20),
        cost_estimate=pl.CostEstimate(
            flops=toks * ranks * depth,
            bytes_accessed=2 * depth * (toks + ranks // 2),
            transcendentals=0,
        ),
    )(*big)


def sketch_kernel(cores, rank_out, bounds, mask, *refs):
    shares, outs = refs[:cores], refs[cores:]
    rows, toks = bounds.shape[0], mask.shape[1]
    rank_in = shares[0].shape[0] - rank_out
    copies = LANES // rank_in
    lane = lax.broadcasted_iota(jnp.int32, (rows, toks), 1)
    inside = (lane >= bounds[:, 0:1]) & (lane < bounds[:, 1:2]) & (mask[...] != 0)
    both = shares[0][...]
    for share in shares[1:]:
        both = both + share[...]
    both = both.astype(jnp.bfloat16)
    g, a = both[:rank_out].astype(jnp.float32), both[rank_out:]
    spread = [jnp.where(inside, g[i : i + 1], 0.0) for i in range(rank_out)]
    weighted = jnp.concatenate(spread, axis=0).astype(jnp.bfloat16)
    total = dot_last(weighted, jnp.concatenate([a] * copies, axis=0))
    column = lax.broadcasted_iota(jnp.int32, (rows, LANES), 1) // rank_in
    flat = []
    for i in range(0, rank_out, copies):
        tile = total[i * rows : (i + 1) * rows]
        for n in range(1, copies):
            tile = jnp.where(column == n, total[(i + n) * rows : (i + n + 1) * rows], tile)
        flat.append(tile)
    sketch = jnp.concatenate(flat, axis=1)
    part = rows // len(outs)
    for n, out in enumerate(outs):
        out[...] = sketch[n * part : (n + 1) * part].astype(out.dtype)


def sketches_of(shares, bounds, mask, rank_out, pair):
    rows = bounds.shape[0]
    depth = rank_out * (shares[0].shape[0] - rank_out)
    return pl.pallas_call(
        functools.partial(sketch_kernel, len(shares), rank_out),
        out_shape=[jax.ShapeDtypeStruct((rows // pair, depth), jnp.bfloat16)] * pair,
        in_specs=[VMEM] * (len(shares) + 2),
        out_specs=[VMEM] * pair,
        compiler_params=pltpu.CompilerParams(vmem_limit_bytes=24 << 20),
        cost_estimate=pl.CostEstimate(
            flops=2 * rows * depth * mask.shape[1],
            bytes_accessed=2 * rows * depth,
            transcendentals=0,
        ),
    )(bounds, mask, *shares)


def score_kernel(count, worker, bounds, *refs):
    sketches, queries, out = refs[:count], refs[count:-1], refs[-1]
    out[...] = jnp.zeros_like(out)

    @pl.when(lax.axis_index("tensor") == worker)
    def _():
        total = sketches[0][...].astype(jnp.float32)
        for sketch in sketches[1:]:
            total = total + sketch[...].astype(jnp.float32)
        total = total.astype(jnp.bfloat16)
        place = bounds[: total.shape[0], 2:3]
        got = [dot_last(total, q[0] if len(q.shape) == 3 else q[...]) for q in queries]
        ordered = []
        for n in range(len(got)):
            pick = got[0]
            for k in range(1, len(got)):
                pick = jnp.where((place ^ k) == n, got[k], pick)
            ordered.append(pick)
        out[...] = jnp.concatenate(ordered, axis=1)


def scores_of(sketches, bounds, queries, worker):
    rows, depth = sketches[0].shape
    width = sum(q.shape[-2] for q in queries)
    return pl.pallas_call(
        functools.partial(score_kernel, len(sketches), worker),
        out_shape=jax.ShapeDtypeStruct((rows, width), jnp.float32),
        in_specs=[VMEM] * (1 + len(sketches) + len(queries)),
        out_specs=VMEM,
        compiler_params=pltpu.CompilerParams(vmem_limit_bytes=24 << 20),
        cost_estimate=pl.CostEstimate(
            flops=2 * rows * depth * width, bytes_accessed=2 * depth * width, transcendentals=0
        ),
    )(bounds, *sketches, *queries)


def to_last(dps, cores, k):
    return [
        (i * cores + c, (i if c else i ^ k) * cores + (c - 1) % cores)
        for i in range(dps)
        for c in range(cores)
    ]


def home_perm(sizes, k):
    dps, layers, cores = sizes
    pair = dps // layers
    perm = []
    for u in range(layers):
        for v in range(pair):
            for l in range(layers):
                src = ((u * pair + v) * layers + l) * cores
                dst = (((l ^ k) * pair + v) * layers + u) * cores
                side = ((u * pair + v) * layers + (l ^ 1)) * cores
                chain = [(src + c, src + c + 1) for c in range(cores - 1)]
                if k or layers != 2:
                    perm += [(src + cores - 1, dst)] + chain
                elif u != l:
                    perm += [(src + cores - 1, dst), (src, side)]
                    perm += [(src + c, src + c + 1) for c in range(1, cores - 1)]
                else:
                    perm += [(src + cores - 1, side + 1)] + chain
    return perm


def hop_order(dps):
    return [1] + list(range(dps - 1, 1, -1))


def local(sizes, activations, out_grads, proj_in, proj_out, queries, lengths, owner_slot, pad_mask):
    dps, layers, cores = sizes
    pair = dps // layers
    assert cores > 1 and dps & (dps - 1) == 0
    toks = activations.shape[1]
    rank_out = proj_out.shape[1]
    own_rows = lengths.shape[0] // dps
    d, l, t = lax.axis_index("dp"), lax.axis_index("layer"), lax.axis_index("tensor")

    v = d % pair

    wanted = [queries]
    for k in range(1, pair):
        wanted.append(lax.ppermute(queries[0], ("dp", "tensor"), to_last(dps, cores, k)))

    partial_sides = project(
        activations, out_grads, proj_in, proj_out
    )
    shares = [partial_sides]
    for k in range(1, cores):
        shares.append(lax.ppermute(partial_sides, "tensor", [(i, i ^ k) for i in range(cores)]))

    rows = layers * own_rows
    index = jnp.arange(pair * rows, dtype=jnp.int32)
    turn = index // rows
    half = l ^ (index % rows // own_rows)
    slot = (half * pair + (v + turn) % pair) * own_rows + index % own_rows
    count = jnp.arange(lengths.shape[0])
    first = jnp.sum(jnp.where(count[None, :] < count[:, None], lengths[None, :], 0), axis=1)
    match = slot[:, None] == owner_slot[None, :]
    low = jnp.sum(jnp.where(match, first[None, :], 0), axis=1) - d * toks
    high = low + jnp.sum(jnp.where(match, lengths[None, :], 0), axis=1)
    column = jnp.arange(3)[None, :]
    bounds = jnp.where(column == 0, low[:, None], jnp.where(column == 1, high[:, None], v))

    sketches = sketches_of(shares, bounds, pad_mask[None], rank_out, pair)

    held = [sketches[0]]
    for k in hop_order(dps):
        perm = [
            (i * cores + c, (i if c else (i + k) % dps) * cores + (c - 1) % cores)
            for i in range(dps)
            for c in range(cores)
        ]
        held.append(lax.ppermute(sketches[k % pair], ("dp", "tensor"), perm))

    served = scores_of(held, bounds, wanted, cores - 1)

    whole = None
    for k in range(layers):
        perm = home_perm(sizes, k)
        piece = served[k * own_rows : (k + 1) * own_rows]
        piece = lax.ppermute(piece, ("dp", "layer", "tensor"), perm)
        if k == 0 and layers == 2:
            piece = jnp.where(d // pair == l, 0.0, piece)
        whole = piece if whole is None else whole + piece
    if layers == 2:
        kept = jnp.where(d // pair == l, served[:own_rows], 0.0)
    else:
        kept = jnp.zeros_like(whole)
    parts = jnp.where(t == 0, whole, jnp.where(t == cores - 1, kept, 0.0))
    result = parts
    for k in range(1, cores):
        result = result + lax.ppermute(
            parts, "tensor", [(i, i ^ k) for i in range(cores)]
        )
    return result


def solution(mesh):
    placed = (
        P("layer", ("groups", "dp"), "tensor"),
        P("layer", ("groups", "dp"), "tensor"),
        P("layer", None, "tensor"),
        P("layer", None, "tensor"),
        P("layer", "dp", None),
        P("groups"),
        P("groups"),
        P(("groups", "dp")),
    )
    sizes = tuple(mesh.shape[name] for name in ("dp", "layer", "tensor"))
    return jax.shard_map(
        functools.partial(local, sizes),
        mesh=mesh,
        in_specs=placed,
        out_specs=P(("groups", "dp"), "layer"),
        check_vma=False,
    )
```
